768 devices in a mesh: row: 16 (over x, y_hi, core), col: 48 (over y_lo, z).
Axes of the slice: x: 4, y: 8 (y_hi: 2, y_lo: 4; y = y_hi * 4 + y_lo), z: 12, core: 2. Of those that a mesh axis runs over, the one named last changes fastest.
Arguments:
- features: bfloat16 [6144, 4096], P('col', 'row'), may hold values from -6 to 6
- weight_blocks: bfloat16 [384, 6, 128, 128], P('col', None, 'row'), may hold values from -0.21875 to 0.21875
- block_rows: int32 [384, 6], P('col'), may hold values from 0 to 47, as said below
- upstream: bfloat16 [49152, 4096], P('col', 'row'), may hold values from -6 to 6
Outputs:
- hidden: bfloat16 [49152, 4096], P('col', 'row')
- input_grad: bfloat16 [6144, 4096], P('col', 'row')
- weight_grad: float32 [384, 6, 128, 128], P('col', None, 'row')
The draws below stay inside these ranges and needn't reach their ends.
Inputs may be any that keep to these rules, and one draw needn't show every extreme that they name: `block_rows`: the 6 block rows of one block column are distinct.
All inputs are finite; a program needn't handle non-finite values.
Results may differ from the reference program's by a relative error of at most 0.0049.
Values may be sent and summed in bfloat16 or wider, within the bound.
A program may use at most 64 MiB of HBM per device.

```python
import jax
import jax.numpy as jnp
from jax import lax

D = 6144
FF = 49152
BLOCK = 128
TOKENS = 4096
DB = 48
FB = 384
KB = 6


def draw_block_rows(key, part):
    subkeys = jax.random.split(key, FB)

    def pick_rows(subkey):
        return jax.random.permutation(subkey, DB)[:KB]
    return jax.vmap(pick_rows)(subkeys).astype(jnp.int32)


def block_scale(key, extent, cuts, low, largest):
    level = 1.0
    for position, shards_of in cuts:
        draws = jax.random.uniform(jax.random.fold_in(jax.random.fold_in(key, 6), position), (shards_of,), jnp.float32, low / len(cuts), largest / len(cuts))
        level = level * jnp.repeat(jnp.exp(draws), extent[position] // shards_of).reshape((-1,) + (1,) * (len(extent) - 1 - position))
    return level


def normal_values(key, dims, scale, reach, shards=(), held_as=jnp.bfloat16):
    drawn = jax.random.normal(key, dims, jnp.float32) * scale
    if len(shards) > 0:
        drawn = block_scale(key, dims, shards, -0.22, 0.18) * drawn
    return jnp.clip(drawn, min=-reach, max=reach).astype(held_as)


def setup_inputs(seed: int = 0) -> dict:
    streams_of = jax.random.split(jax.random.key(seed), 5)
    features = normal_values(streams_of[0], (D, TOKENS), 1.0, 6.0, ((0, 48), (1, 16)))
    weight_blocks = normal_values(streams_of[1], (FB, KB, BLOCK, BLOCK), (KB * BLOCK) ** -0.5, 0.21875, ((0, 48), (2, 16)))
    block_rows = draw_block_rows(jax.random.fold_in(streams_of[4], 71), 0)
    upstream = normal_values(streams_of[3], (FF, TOKENS), 1.0, 6.0, ((0, 48), (1, 16)))
    return {"features": features, "weight_blocks": weight_blocks, "block_rows": block_rows, "upstream": upstream}


def reference(features, weight_blocks, block_rows, upstream):
    tok_count = features.shape[1]
    blocks = features.reshape(DB, BLOCK, tok_count)
    grad_up = upstream.reshape(FB, BLOCK, tok_count)
    grad_scale = float(TOKENS) ** (-0.5)

    def column(carry, items):
        weights, rows, upper = items
        rows = rows.astype(jnp.int32)
        picked = blocks[rows].astype(jnp.float32)
        weights = weights.astype(jnp.float32)
        preact = jnp.einsum('skt,skn->nt', picked, weights, precision=lax.Precision.HIGHEST)
        hidden = jax.nn.gelu(preact).astype(jnp.bfloat16)
        _, pullback = jax.vjp(jax.nn.gelu, preact)
        grad_pre = pullback(upper.astype(jnp.float32))[0].astype(jnp.bfloat16)
        grad_wide = grad_pre.astype(jnp.float32)
        input_part = jnp.einsum('nt,skn->skt', grad_wide, weights, precision=lax.Precision.HIGHEST)
        weight_grad = jnp.einsum('skt,nt->skn', picked, grad_wide, precision=lax.Precision.HIGHEST) * grad_scale
        carry = carry.at[rows].add(input_part)
        return (carry, (hidden, weight_grad))
    initial = jnp.zeros((DB, BLOCK, tok_count), jnp.float32)
    total, outputs = lax.scan(column, initial, (weight_blocks, block_rows, grad_up))
    hidden, weight_grad = outputs
    return (hidden.reshape(FF, tok_count), total.reshape(D, tok_count).astype(jnp.bfloat16), weight_grad)
```

```python
import functools
import math

import jax
import jax.numpy as jnp
from jax import lax
from jax.experimental import pallas as pl
from jax.experimental.pallas import tpu as pltpu
from jax.sharding import PartitionSpec as P

Y, Z = 4, 12
X = 4
HALF_RING = Z // 2
PLUS, MINUS = 0, 1
VMEM = pltpu.VMEM


def places():
    col = lax.axis_index("col")
    row = lax.axis_index("row")
    y, z = col // Z, col % Z
    x, h, core = row // 4, (row // 2) % 2, row % 2

    def col_of(dy, dz):
        return ((y + dy + Y) % Y) * Z + (z + dz + Z) % Z

    def row_of(dx, dh, dc):
        return (((x + dx + X) % X) * 2 + (h + dh) % 2) * 2 + (core + dc) % 2

    return col_of, row_of


def enter(col_of, row_of):
    barrier = pltpu.get_barrier_semaphore()
    cols = [col_of(1, 0), col_of(2, 0), col_of(3, 0), col_of(0, 1), col_of(0, -1)]
    rows = [row_of(0, 0, 1), row_of(0, 1, 0), row_of(1, 0, 0), row_of(-1, 0, 0)]
    for c in cols:
        pl.semaphore_signal(barrier, inc=1, device_id={"col": c})
    for r in rows:
        pl.semaphore_signal(barrier, inc=1, device_id={"row": r})
    pl.semaphore_wait(barrier, len(cols) + len(rows))


def gather_kernel(feat, wts, feat_all, wts_all, ys, yr, zs, zr, ws, wr):
    col_of, row_of = places()
    me_col, me_row = col_of(0, 0), row_of(0, 0, 0)
    half = feat.shape[0] // 2
    started = []

    def send(src, dst, send_sem, recv_sem, **to):
        copy = pltpu.make_async_remote_copy(
            src_ref=src, dst_ref=dst, send_sem=send_sem, recv_sem=recv_sem, device_id=to
        )
        copy.start()
        started.append(copy)
        return copy

    def send_w(i, slot, src, to):
        return send(src, wts_all.at[slot], ws.at[i], wr.at[i], row=to)

    def send_z(way, k, j):
        step = 1 if way == PLUS else -1
        slot = col_of(j, -step * (k - 1))
        src = feat if (j == 0 and k == 1) else feat_all.at[slot]
        dst = feat_all.at[slot]
        if k == HALF_RING:
            part = pl.ds(0, half) if way == PLUS else pl.ds(half, half)
            src, dst = src.at[part], dst.at[part]
        return send(src, dst, zs.at[way, k - 1, j], zr.at[way, k - 1, j], col=col_of(0, step))

    enter(col_of, row_of)
    core_to, h_to = row_of(0, 0, 1), row_of(0, 1, 0)
    x_up, x_down = row_of(1, 0, 0), row_of(-1, 0, 0)

    zc = {}
    yc = {}
    for way in (PLUS, MINUS):
        zc[way, 1, 0] = send_z(way, 1, 0)
    for j in (1, 3, 2):
        yc[j] = send(feat, feat_all.at[me_col], ys.at[j - 1], yr.at[j - 1], col=col_of(4 - j, 0))
    w_h = send_w(0, me_row, wts, h_to)
    w_up = send_w(1, me_row, wts, x_up)
    w_down = send_w(2, me_row, wts, x_down)
    cores = [send_w(7, me_row, wts, core_to)]
    feat_all[me_col] = feat[...]
    wts_all[me_row] = wts[...]

    def w_stage_x():
        w_up.wait_recv()
        slot = row_of(-1, 0, 0)
        first = send_w(3, slot, wts_all.at[slot], x_up)
        cores.append(send_w(8, slot, wts_all.at[slot], core_to))
        w_down.wait_recv()
        slot = row_of(1, 0, 0)
        cores.append(send_w(9, slot, wts_all.at[slot], core_to))
        w_h.wait_recv()
        slot = row_of(0, 1, 0)
        up = send_w(4, slot, wts_all.at[slot], x_up)
        down = send_w(5, slot, wts_all.at[slot], x_down)
        cores.append(send_w(10, slot, wts_all.at[slot], core_to))
        return first, up, down

    def w_stage_far(first, up, down):
        down.wait_recv()
        slot = row_of(1, 1, 0)
        last = send_w(6, slot, wts_all.at[slot], x_down)
        cores.append(send_w(11, slot, wts_all.at[slot], core_to))
        up.wait_recv()
        slot = row_of(-1, 1, 0)
        cores.append(send_w(12, slot, wts_all.at[slot], core_to))
        first.wait_recv()
        slot = row_of(2, 0, 0)
        cores.append(send_w(13, slot, wts_all.at[slot], core_to))
        return last

    def w_stage_last(last):
        last.wait_recv()
        slot = row_of(2, 1, 0)
        cores.append(send_w(14, slot, wts_all.at[slot], core_to))

    for j in (1, 3, 2):
        yc[j].wait_recv()
        for way in (PLUS, MINUS):
            zc[way, 1, j] = send_z(way, 1, j)
    pending = None
    for k in range(2, HALF_RING + 1):
        for j in (0, 1, 3, 2):
            for way in (PLUS, MINUS):
                zc[way, k - 1, j].wait_recv()
                zc[way, k, j] = send_z(way, k, j)
        if k == 2:
            pending = w_stage_x()
        elif k == 3:
            pending = w_stage_far(*pending)
        elif k == 4:
            w_stage_last(pending)
    for copy in cores:
        copy.wait_recv()
    for j in range(Y):
        for way in (PLUS, MINUS):
            zc[way, HALF_RING, j].wait_recv()
    for copy in started:
        copy.wait_send()


def gather(features, weights):
    dma = pltpu.SemaphoreType.DMA
    return pl.pallas_call(
        gather_kernel,
        out_shape=(
            jax.ShapeDtypeStruct((Y * Z,) + features.shape, features.dtype),
            jax.ShapeDtypeStruct((X * 4,) + weights.shape, weights.dtype),
        ),
        in_specs=[pl.BlockSpec(memory_space=VMEM)] * 2,
        out_specs=(pl.BlockSpec(memory_space=VMEM),) * 2,
        scratch_shapes=[
            dma((Y - 1,)), dma((Y - 1,)),
            dma((2, HALF_RING, Y)), dma((2, HALF_RING, Y)),
            dma((15,)), dma((15,)),
        ],
        compiler_params=pltpu.CompilerParams(collective_id=1, has_side_effects=True),
        name="gather_features_weights",
    )(features, weights)


def compute_kernel(rows, blocks, wts, upper, hidden, in_part, w_part):
    in_part[...] = jnp.zeros_like(in_part)
    c = math.sqrt(2.0 / math.pi)
    cols, slots = wts.shape[0], wts.shape[1]
    n_owner = w_part.shape[0]
    for f in range(cols):
        at = [rows[f, s] for s in range(slots)]
        picked = jnp.concatenate([blocks[a] for a in at], axis=0)
        w = wts[f].reshape(slots * 128, 128)
        v = lax.dot_general(w, picked, (((0,), (0,)), ((), ())), preferred_element_type=jnp.float32)
        sq = v * v
        t = jnp.tanh(c * (v + 0.044715 * (sq * v)))
        gate = 0.5 * (1.0 + t)
        here = pl.ds(f * 128, 128)
        hidden[here, :] = (v * gate).astype(jnp.bfloat16)
        slope = gate + 0.5 * v * (1.0 - t * t) * (c * (1.0 + (3 * 0.044715) * sq))
        g = (upper[here, :].astype(jnp.float32) * slope).astype(jnp.bfloat16)
        part = jnp.dot(w, g, preferred_element_type=jnp.float32)
        for s in range(slots):
            in_part[at[s]] += part[s * 128 : (s + 1) * 128]
        wg = lax.dot_general(picked, g, (((1,), (1,)), ((), ())), preferred_element_type=jnp.float32)
        for s in range(slots):
            w_part[:, pl.ds((f * slots + s) * 8, 8), :] = wg[s * 128 : (s + 1) * 128].reshape(
                n_owner, 8, 128
            )


def compute(rows, blocks, wts, upper):
    f, s = rows.shape
    return pl.pallas_call(
        compute_kernel,
        out_shape=(
            jax.ShapeDtypeStruct(upper.shape, jnp.bfloat16),
            jax.ShapeDtypeStruct(blocks.shape, jnp.float32),
            jax.ShapeDtypeStruct((X * 4, f * s * 8, 128), jnp.float32),
        ),
        in_specs=[pl.BlockSpec(memory_space=pltpu.SMEM)] + [pl.BlockSpec(memory_space=VMEM)] * 3,
        out_specs=(pl.BlockSpec(memory_space=VMEM),) * 3,
        name="block_columns",
    )(rows, blocks, wts, upper)


def reduce_kernel(
    scale, in_part, w_part, in_out, w_out,
    zbuf_s, zbuf_r, ybuf_s, ybuf_r, cbuf_s, cbuf_r, own, xbuf_s, xbuf_r,
    zs, zr, ys, yr, cs, cr, xs, xr,
):
    col_of, row_of = places()
    half = in_part.shape[1] // 2
    f32, bf16 = jnp.float32, jnp.bfloat16
    started = []
    order = (2, 1, 3, 0)

    def send(src, dst, send_sem, recv_sem, **to):
        copy = pltpu.make_async_remote_copy(
            src_ref=src, dst_ref=dst, send_sem=send_sem, recv_sem=recv_sem, device_id=to
        )
        copy.start()
        started.append(copy)
        return copy

    def send_z(way, k, j):
        step = 1 if way == PLUS else -1
        src, dst = zbuf_s.at[way, k, j], zbuf_r.at[way, k, j]
        if k == 0:
            part = pl.ds(0, half) if way == PLUS else pl.ds(half, half)
            src, dst = src.at[part], dst.at[part]
        return send(src, dst, zs.at[way, k, j], zr.at[way, k, j], col=col_of(0, step))

    def send_x(i, to):
        return send(xbuf_s.at[i], xbuf_r.at[i], xs.at[i], xr.at[i], row=to)

    enter(col_of, row_of)
    core_to, h_to = row_of(0, 0, 1), row_of(0, 1, 0)
    x_up, x_down = row_of(1, 0, 0), row_of(-1, 0, 0)

    zc = {}
    for j in order:
        far = col_of(j, HALF_RING)
        for way in (PLUS, MINUS):
            part = pl.ds(0, half) if way == PLUS else pl.ds(half, half)
            zbuf_s[way, 0, j, part, :] = in_part[far, part, :].astype(bf16)
            zc[way, 0, j] = send_z(way, 0, j)

    dests = [(2, 0), (2, 1), (1, 0), (1, 1), (-1, 0), (-1, 1), (0, 1), (0, 0)]
    cc = []
    for i, (dx, dh) in enumerate(dests):
        cbuf_s[i] = w_part[row_of(dx, dh, 1)].astype(bf16)
        cc.append(send(cbuf_s.at[i], cbuf_r.at[i], cs.at[i], cr.at[i], row=core_to))

    def pair(i):
        dx, dh = dests[i]
        cc[i].wait_recv()
        return w_part[row_of(dx, dh, 0)] + cbuf_r[i].astype(f32)

    xc = {}

    def w_far():
        xbuf_s[0] = pair(0).astype(bf16)
        xc[0] = send_x(0, x_up)
        xbuf_s[1] = pair(1).astype(bf16)
        xc[1] = send_x(1, x_down)
        xbuf_s[2] = pair(3).astype(bf16)
        xc[2] = send_x(2, x_up)
        xbuf_s[3] = pair(4).astype(bf16)
        xc[3] = send_x(3, x_down)

    def w_near():
        xc[0].wait_recv()
        xbuf_s[4] = (pair(2) + xbuf_r[0].astype(f32)).astype(bf16)
        xc[4] = send_x(4, x_up)
        xc[1].wait_recv()
        xbuf_s[5] = (pair(5) + xbuf_r[1].astype(f32)).astype(bf16)
        xc[5] = send_x(5, x_down)
        own[...] = pair(7)

    def w_across():
        xc[2].wait_recv()
        xc[5].wait_recv()
        total = pair(6) + xbuf_r[2].astype(f32) + xbuf_r[5].astype(f32)
        xbuf_s[6] = total.astype(bf16)
        xc[6] = send_x(6, h_to)

    def w_end():
        xc[3].wait_recv()
        xc[4].wait_recv()
        xc[6].wait_recv()
        total = own[...] + xbuf_r[3].astype(f32) + xbuf_r[4].astype(f32) + xbuf_r[6].astype(f32)
        w_out[...] = total * scale

    def add_z(way, k, j):
        step = 1 if way == PLUS else -1
        slot = col_of(j, step * (HALF_RING - k))
        zc[way, k - 1, j].wait_recv()
        if k > 1:
            zbuf_s[way, k, j] = (in_part[slot] + zbuf_r[way, k - 1, j].astype(f32)).astype(bf16)
            return
        got = pl.ds(0, half) if way == PLUS else pl.ds(half, half)
        rest = pl.ds(half, half) if way == PLUS else pl.ds(0, half)
        zbuf_s[way, k, j, got, :] = (
            in_part[slot, got, :] + zbuf_r[way, 0, j, got, :].astype(f32)
        ).astype(bf16)
        zbuf_s[way, k, j, rest, :] = in_part[slot, rest, :].astype(bf16)

    stages = {1: w_far, 2: w_near, 3: w_across, 4: w_end}
    for k in range(1, HALF_RING):
        for j in order:
            for way in (PLUS, MINUS):
                add_z(way, k, j)
                zc[way, k, j] = send_z(way, k, j)
        if k in stages:
            stages[k]()

    def total_z(j):
        for way in (PLUS, MINUS):
            zc[way, HALF_RING - 1, j].wait_recv()
        return (
            in_part[col_of(j, 0)]
            + zbuf_r[PLUS, HALF_RING - 1, j].astype(f32)
            + zbuf_r[MINUS, HALF_RING - 1, j].astype(f32)
        )

    yc = []
    for j in (2, 1, 3):
        ybuf_s[j - 1] = total_z(j).astype(bf16)
        yc.append(
            send(ybuf_s.at[j - 1], ybuf_r.at[j - 1], ys.at[j - 1], yr.at[j - 1], col=col_of(j, 0))
        )
    total = total_z(0)
    for copy in yc:
        copy.wait_recv()
    for j in range(Y - 1):
        total = total + ybuf_r[j].astype(f32)
    in_out[...] = total.astype(bf16)
    for copy in started:
        copy.wait_send()


def reduce(in_part, w_part, scale):
    dma = pltpu.SemaphoreType.DMA
    block, piece = in_part.shape[1:], w_part.shape[1:]
    bf16 = jnp.bfloat16
    return pl.pallas_call(
        functools.partial(reduce_kernel, scale),
        out_shape=(
            jax.ShapeDtypeStruct(block, bf16),
            jax.ShapeDtypeStruct(piece, jnp.float32),
        ),
        in_specs=[pl.BlockSpec(memory_space=VMEM)] * 2,
        out_specs=(pl.BlockSpec(memory_space=VMEM),) * 2,
        scratch_shapes=[
            VMEM((2, HALF_RING, Y) + block, bf16), VMEM((2, HALF_RING, Y) + block, bf16),
            VMEM((Y - 1,) + block, bf16), VMEM((Y - 1,) + block, bf16),
            VMEM((8,) + piece, bf16), VMEM((8,) + piece, bf16),
            VMEM(piece, jnp.float32),
            VMEM((7,) + piece, bf16), VMEM((7,) + piece, bf16),
            dma((2, HALF_RING, Y)), dma((2, HALF_RING, Y)),
            dma((Y - 1,)), dma((Y - 1,)),
            dma((8,)), dma((8,)),
            dma((7,)), dma((7,)),
        ],
        compiler_params=pltpu.CompilerParams(collective_id=2, has_side_effects=True),
        name="reduce_gradients",
    )(in_part, w_part)


def local(features, weight_blocks, block_rows, upstream):
    cols, slots, rows_here, n = weight_blocks.shape
    grad_scale = float(features.shape[1] * lax.axis_size("row")) ** (-0.5)
    blocks, pieces = gather(features, weight_blocks.reshape(-1, n))
    weights = (
        pieces.reshape(-1, cols, slots, rows_here, n)
        .transpose(1, 2, 0, 3, 4)
        .reshape(cols, slots, -1, n)
    )
    hidden, in_part, w_part = compute(block_rows, blocks, weights, upstream)
    input_grad, w_grad = reduce(in_part, w_part, grad_scale)
    return (hidden, input_grad, w_grad.reshape(weight_blocks.shape))


def solution(mesh):
    return jax.shard_map(
        local,
        mesh=mesh,
        in_specs=(P("col", "row"), P("col", None, "row", None), P("col", None), P("col", "row")),
        out_specs=(P("col", "row"), P("col", "row"), P("col", None, "row", None)),
        check_vma=False,
    )
```

```python
import functools
import math

import jax
import jax.numpy as jnp
from jax import lax
from jax.experimental import pallas as pl
from jax.experimental.pallas import tpu as pltpu
from jax.sharding import PartitionSpec as P

Y, Z = 4, 12
X = 4
HALF_RING = Z // 2
PLUS, MINUS = 0, 1
VMEM = pltpu.VMEM


def places():
    col = lax.axis_index("col")
    row = lax.axis_index("row")
    y, z = col // Z, col % Z
    x, h, core = row // 4, (row // 2) % 2, row % 2

    def col_of(dy, dz):
        return ((y + dy + Y) % Y) * Z + (z + dz + Z) % Z

    def row_of(dx, dh, dc):
        return (((x + dx + X) % X) * 2 + (h + dh) % 2) * 2 + (core + dc) % 2

    return col_of, row_of


def enter(col_of, row_of):
    barrier = pltpu.get_barrier_semaphore()
    cols = [col_of(1, 0), col_of(2, 0), col_of(3, 0), col_of(0, 1), col_of(0, -1)]
    rows = [row_of(0, 0, 1), row_of(0, 1, 0), row_of(1, 0, 0), row_of(-1, 0, 0)]
    for c in cols:
        pl.semaphore_signal(barrier, inc=1, device_id={"col": c})
    for r in rows:
        pl.semaphore_signal(barrier, inc=1, device_id={"row": r})
    pl.semaphore_wait(barrier, len(cols) + len(rows))


def step_kernel(
    scale, rows, feat, wts, upper, hidden, in_out, w_out,
    feat_all, wts_all, places_of, grad, term, w_part,
    zbuf_s, zbuf_r, ybuf_s, ybuf_r, cbuf_s, cbuf_r, own, xbuf_s, xbuf_r,
    gys, gyr, gzs, gzr, gws, gwr, local_sem,
    zs, zr, ys, yr, cs, cr, xs, xr,
):
    col_of, row_of = places()
    me_col, me_row = col_of(0, 0), row_of(0, 0, 0)
    half = feat.shape[0] // 2
    f32, bf16 = jnp.float32, jnp.bfloat16
    columns, slots = rows.shape
    no_block = columns * slots
    started = []

    def send(src, dst, send_sem, recv_sem, **to):
        copy = pltpu.make_async_remote_copy(
            src_ref=src, dst_ref=dst, send_sem=send_sem, recv_sem=recv_sem, device_id=to
        )
        copy.start()
        started.append(copy)
        return copy

    def w_at(slot):
        return wts_all.at[pl.ds(0, no_block), pl.ds(pl.multiple_of(slot * 8, 8), 8), :]

    def gather_w(i, slot, to, src=None):
        return send(w_at(slot) if src is None else src, w_at(slot), gws.at[i], gwr.at[i], row=to)

    def gather_z(way, k, j):
        step = 1 if way == PLUS else -1
        slot = col_of(j, -step * (k - 1))
        src = feat if (j == 0 and k == 1) else feat_all.at[slot]
        dst = feat_all.at[slot]
        if k == HALF_RING:
            part = pl.ds(0, half) if way == PLUS else pl.ds(half, half)
            src, dst = src.at[part], dst.at[part]
        return send(src, dst, gzs.at[way, k - 1, j], gzr.at[way, k - 1, j], col=col_of(0, step))

    enter(col_of, row_of)
    core_to, h_to = row_of(0, 0, 1), row_of(0, 1, 0)
    x_up, x_down = row_of(1, 0, 0), row_of(-1, 0, 0)

    zc = {}
    yc = {}
    for way in (PLUS, MINUS):
        zc[way, 1, 0] = gather_z(way, 1, 0)
    for j in (1, 3, 2):
        yc[j] = send(feat, feat_all.at[me_col], gys.at[j - 1], gyr.at[j - 1], col=col_of(4 - j, 0))
    w_h = gather_w(0, me_row, h_to, wts)
    w_up = gather_w(1, me_row, x_up, wts)
    w_down = gather_w(2, me_row, x_down, wts)
    cores = [gather_w(7, me_row, core_to, wts)]
    mine = pltpu.make_async_copy(wts, w_at(me_row), local_sem)
    mine.start()
    feat_all[me_col] = feat[...]
    wts_all[no_block] = jnp.zeros_like(wts_all[no_block])

    def w_stage_x():
        w_up.wait_recv()
        slot = row_of(-1, 0, 0)
        first = gather_w(3, slot, x_up)
        cores.append(gather_w(8, slot, core_to))
        w_down.wait_recv()
        cores.append(gather_w(9, row_of(1, 0, 0), core_to))
        w_h.wait_recv()
        slot = row_of(0, 1, 0)
        up = gather_w(4, slot, x_up)
        down = gather_w(5, slot, x_down)
        cores.append(gather_w(10, slot, core_to))
        return first, up, down

    def w_stage_far(first, up, down):
        down.wait_recv()
        slot = row_of(1, 1, 0)
        last = gather_w(6, slot, x_down)
        cores.append(gather_w(11, slot, core_to))
        up.wait_recv()
        cores.append(gather_w(12, row_of(-1, 1, 0), core_to))
        first.wait_recv()
        cores.append(gather_w(13, row_of(2, 0, 0), core_to))
        return last

    def w_stage_last(last):
        last.wait_recv()
        cores.append(gather_w(14, row_of(2, 1, 0), core_to))

    def find_blocks(b, carry):
        for f in range(columns):
            found = jnp.int32(no_block)
            for s in range(slots):
                found = jnp.where(rows[f, s] == b, jnp.int32(f * slots + s), found)
            places_of[b, f] = found
        return carry

    third = Y * Z // 4
    for j in (1, 3, 2):
        yc[j].wait_recv()
        for way in (PLUS, MINUS):
            zc[way, 1, j] = gather_z(way, 1, j)
    pending = None
    for k in range(2, HALF_RING + 1):
        for j in (0, 1, 3, 2):
            for way in (PLUS, MINUS):
                zc[way, k - 1, j].wait_recv()
                zc[way, k, j] = gather_z(way, k, j)
        if k == 2:
            pending = w_stage_x()
        elif k == 3:
            pending = w_stage_far(*pending)
        elif k == 4:
            w_stage_last(pending)
        if k < HALF_RING:
            lax.fori_loop((k - 2) * third, (k - 1) * third, find_blocks, 0)
    mine.wait()
    for copy in cores:
        copy.wait_recv()
    for j in range(Y):
        for way in (PLUS, MINUS):
            zc[way, HALF_RING, j].wait_recv()

    def pick(f):
        return jnp.concatenate([feat_all[rows[f, s]] for s in range(slots)], axis=0)

    c = math.sqrt(2.0 / math.pi)
    for f in range(columns):
        w = wts_all[f * slots : (f + 1) * slots].reshape(slots * 128, 128)
        v = lax.dot_general(w, pick(f), (((0,), (0,)), ((), ())), preferred_element_type=f32)
        sq = v * v
        t = jnp.tanh(c * (v + 0.044715 * (sq * v)))
        gate = 0.5 * (1.0 + t)
        here = pl.ds(f * 128, 128)
        hidden[here, :] = (v * gate).astype(bf16)
        slope = gate + 0.5 * v * (1.0 - t * t) * (c * (1.0 + (3 * 0.044715) * sq))
        grad[here, :] = (upper[here, :].astype(f32) * slope).astype(bf16)

    order = (2, 1, 3, 0)

    def terms(i, dz):
        left = []
        for j in order:
            b = col_of(j, dz)
            left.append(
                jnp.concatenate([wts_all[places_of[b, f]] for f in range(columns)], axis=1)
            )
        term[i] = jnp.dot(jnp.concatenate(left, axis=0), grad[...], preferred_element_type=f32)

    def term_of(i, j, start=0, size=128):
        return term[i, pl.ds(order.index(j) * 128 + start, size), :]

    def send_z(way, k, j):
        step = 1 if way == PLUS else -1
        src, dst = zbuf_s.at[way, k, j], zbuf_r.at[way, k, j]
        if k == 0:
            part = pl.ds(0, half) if way == PLUS else pl.ds(half, half)
            src, dst = src.at[part], dst.at[part]
        return send(src, dst, zs.at[way, k, j], zr.at[way, k, j], col=col_of(0, step))

    def send_x(i, to):
        return send(xbuf_s.at[i], xbuf_r.at[i], xs.at[i], xr.at[i], row=to)

    zc = {}
    terms(PLUS, HALF_RING)
    for j in order:
        for way in (PLUS, MINUS):
            first = 0 if way == PLUS else half
            zbuf_s[way, 0, j, pl.ds(first, half), :] = term_of(PLUS, j, first, half).astype(bf16)
            zc[way, 0, j] = send_z(way, 0, j)

    for f in range(columns):
        wg = lax.dot_general(
            pick(f), grad[pl.ds(f * 128, 128), :], (((1,), (1,)), ((), ())),
            preferred_element_type=f32,
        )
        for s in range(slots):
            w_part[:, pl.ds((f * slots + s) * 8, 8), :] = wg[s * 128 : (s + 1) * 128].reshape(
                X * 4, 8, 128
            )

    dests = [(2, 0), (2, 1), (1, 0), (1, 1), (-1, 0), (-1, 1), (0, 1), (0, 0)]
    cc = []
    for i, (dx, dh) in enumerate(dests):
        cbuf_s[i] = w_part[row_of(dx, dh, 1)].astype(bf16)
        cc.append(send(cbuf_s.at[i], cbuf_r.at[i], cs.at[i], cr.at[i], row=core_to))

    def pair(i):
        dx, dh = dests[i]
        cc[i].wait_recv()
        return w_part[row_of(dx, dh, 0)] + cbuf_r[i].astype(f32)

    xc = {}

    def w_far():
        xbuf_s[0] = pair(0).astype(bf16)
        xc[0] = send_x(0, x_up)
        xbuf_s[1] = pair(1).astype(bf16)
        xc[1] = send_x(1, x_down)
        xbuf_s[2] = pair(3).astype(bf16)
        xc[2] = send_x(2, x_up)
        xbuf_s[3] = pair(4).astype(bf16)
        xc[3] = send_x(3, x_down)

    def w_near():
        xc[0].wait_recv()
        xbuf_s[4] = (pair(2) + xbuf_r[0].astype(f32)).astype(bf16)
        xc[4] = send_x(4, x_up)
        xc[1].wait_recv()
        xbuf_s[5] = (pair(5) + xbuf_r[1].astype(f32)).astype(bf16)
        xc[5] = send_x(5, x_down)
        own[...] = pair(7)

    def w_across():
        xc[2].wait_recv()
        xc[5].wait_recv()
        total = pair(6) + xbuf_r[2].astype(f32) + xbuf_r[5].astype(f32)
        xbuf_s[6] = total.astype(bf16)
        xc[6] = send_x(6, h_to)

    def w_end():
        xc[3].wait_recv()
        xc[4].wait_recv()
        xc[6].wait_recv()
        total = own[...] + xbuf_r[3].astype(f32) + xbuf_r[4].astype(f32) + xbuf_r[6].astype(f32)
        w_out[...] = total * scale

    def add_z(way, k, j):
        zc[way, k - 1, j].wait_recv()
        if k > 1:
            zbuf_s[way, k, j] = (
                term_of(way, j) + zbuf_r[way, k - 1, j].astype(f32)
            ).astype(bf16)
            return
        got, rest = (0, half) if way == PLUS else (half, 0)
        zbuf_s[way, k, j, pl.ds(got, half), :] = (
            term_of(way, j, got, half) + zbuf_r[way, 0, j, pl.ds(got, half), :].astype(f32)
        ).astype(bf16)
        zbuf_s[way, k, j, pl.ds(rest, half), :] = term_of(way, j, rest, half).astype(bf16)

    stages = {1: w_far, 2: w_near, 3: w_across, 4: w_end}
    for k in range(1, HALF_RING):
        terms(PLUS, HALF_RING - k)
        terms(MINUS, k - HALF_RING)
        for j in order:
            for way in (PLUS, MINUS):
                add_z(way, k, j)
                zc[way, k, j] = send_z(way, k, j)
        if k in stages:
            stages[k]()
    terms(PLUS, 0)

    def total_z(j):
        for way in (PLUS, MINUS):
            zc[way, HALF_RING - 1, j].wait_recv()
        return (
            term_of(PLUS, j)
            + zbuf_r[PLUS, HALF_RING - 1, j].astype(f32)
            + zbuf_r[MINUS, HALF_RING - 1, j].astype(f32)
        )

    yc = []
    for j in (2, 1, 3):
        ybuf_s[j - 1] = total_z(j).astype(bf16)
        yc.append(
            send(ybuf_s.at[j - 1], ybuf_r.at[j - 1], ys.at[j - 1], yr.at[j - 1], col=col_of(j, 0))
        )
    total = total_z(0)
    for copy in yc:
        copy.wait_recv()
    for j in range(Y - 1):
        total = total + ybuf_r[j].astype(f32)
    in_out[...] = total.astype(bf16)
    for copy in started:
        copy.wait_send()


def step(rows, features, weights, upper, scale):
    dma = pltpu.SemaphoreType.DMA
    bf16, f32 = jnp.bfloat16, jnp.float32
    block = features.shape
    pieces, side, n = weights.shape
    columns = rows.shape[0]
    piece = (pieces * side, n)
    ring = (2, HALF_RING, Y)
    vmem = pl.BlockSpec(memory_space=VMEM)
    return pl.pallas_call(
        functools.partial(step_kernel, scale),
        out_shape=(
            jax.ShapeDtypeStruct(upper.shape, bf16),
            jax.ShapeDtypeStruct(block, bf16),
            jax.ShapeDtypeStruct(piece, f32),
        ),
        in_specs=[pl.BlockSpec(memory_space=pltpu.SMEM), vmem, vmem, vmem],
        out_specs=(vmem,) * 3,
        scratch_shapes=[
            VMEM((Y * Z,) + block, bf16),
            VMEM((pieces + 1, X * 4 * side, n), bf16),
            pltpu.SMEM((Y * Z, columns), jnp.int32),
            VMEM(upper.shape, bf16),
            VMEM((2, Y * block[0], block[1]), f32),
            VMEM((X * 4,) + piece, f32),
            VMEM(ring + block, bf16), VMEM(ring + block, bf16),
            VMEM((Y - 1,) + block, bf16), VMEM((Y - 1,) + block, bf16),
            VMEM((8,) + piece, bf16), VMEM((8,) + piece, bf16),
            VMEM(piece, f32),
            VMEM((7,) + piece, bf16), VMEM((7,) + piece, bf16),
            dma((Y - 1,)), dma((Y - 1,)),
            dma(ring), dma(ring),
            dma((15,)), dma((15,)),
            dma,
            dma(ring), dma(ring),
            dma((Y - 1,)), dma((Y - 1,)),
            dma((8,)), dma((8,)),
            dma((7,)), dma((7,)),
        ],
        compiler_params=pltpu.CompilerParams(collective_id=1, has_side_effects=True),
        name="layer_and_gradients",
    )(rows, features, weights, upper)


def finish_kernel(hidden, in_grad, w_grad, hidden_out, in_out, w_out):
    hidden_out[...] = hidden[...]
    in_out[...] = in_grad[...]
    w_out[...] = w_grad[...]


def finish(*arrays):
    return pl.pallas_call(
        finish_kernel,
        out_shape=tuple(jax.ShapeDtypeStruct(a.shape, a.dtype) for a in arrays),
        in_specs=[pl.BlockSpec(memory_space=VMEM)] * 3,
        out_specs=(pl.BlockSpec(memory_space=VMEM),) * 3,
        name="outputs",
    )(*arrays)


def local(features, weight_blocks, block_rows, upstream):
    grad_scale = float(features.shape[1] * lax.axis_size("row")) ** (-0.5)
    weights = weight_blocks.reshape((-1,) + weight_blocks.shape[2:])
    hidden, input_grad, w_grad = finish(
        *step(block_rows, features, weights, upstream, grad_scale)
    )
    return (hidden, input_grad, w_grad.reshape(weight_blocks.shape))


def solution(mesh):
    return jax.shard_map(
        local,
        mesh=mesh,
        in_specs=(P("col", "row"), P("col", None, "row", None), P("col", None), P("col", "row")),
        out_specs=(P("col", "row"), P("col", "row"), P("col", None, "row", None)),
        check_vma=False,
    )
```

```python
import functools
import math

import jax
import jax.numpy as jnp
from jax import lax
from jax.experimental import pallas as pl
from jax.experimental.pallas import tpu as pltpu
from jax.sharding import PartitionSpec as P

Y, Z = 4, 12
X = 4
HALF_RING = Z // 2
PLUS, MINUS = 0, 1
SPREAD = 32
VMEM = pltpu.VMEM


def places():
    col = lax.axis_index("col")
    row = lax.axis_index("row")
    y, z = col // Z, col % Z
    x, h, core = row // 4, (row // 2) % 2, row % 2

    def col_of(dy, dz):
        return ((y + dy + Y) % Y) * Z + (z + dz + Z) % Z

    def row_of(dx, dh, dc):
        return (((x + dx + X) % X) * 2 + (h + dh) % 2) * 2 + (core + dc) % 2

    return col_of, row_of


def enter(col_of, row_of):
    barrier = pltpu.get_barrier_semaphore()
    cols = [col_of(1, 0), col_of(2, 0), col_of(3, 0), col_of(0, 1), col_of(0, -1)]
    rows = [row_of(0, 0, 1), row_of(0, 1, 0), row_of(1, 0, 0), row_of(-1, 0, 0)]
    for c in cols:
        pl.semaphore_signal(barrier, inc=1, device_id={"col": c})
    for r in rows:
        pl.semaphore_signal(barrier, inc=1, device_id={"row": r})
    pl.semaphore_wait(barrier, len(cols) + len(rows))


def step_kernel(
    scale, rows, feat, wts, upper, hidden, in_out, w_out,
    feat_all, wts_all, places_of, grad, term, w_part,
    zbuf_s, zbuf_r, ybuf_s, ybuf_r, cbuf_s, cbuf_r, own, xbuf_s, xbuf_r,
    sbuf_s, sbuf_r,
    gys, gyr, gzs, gzr, gws, gwr, gss, gsr, local_sem,
    zs, zr, ys, yr, cs, cr, xs, xr, ss, sr,
):
    col_of, row_of = places()
    me_col, me_row = col_of(0, 0), row_of(0, 0, 0)
    whole = feat.shape[0]
    ringed = whole - SPREAD
    f32, bf16 = jnp.float32, jnp.bfloat16
    columns, slots = rows.shape
    no_block = columns * slots
    started = []

    def send(src, dst, send_sem, recv_sem, **to):
        copy = pltpu.make_async_remote_copy(
            src_ref=src, dst_ref=dst, send_sem=send_sem, recv_sem=recv_sem, device_id=to
        )
        copy.start()
        started.append(copy)
        return copy

    def height(j):
        return whole if j == 0 else ringed

    def share(way, j):
        cut = min(whole // 2, height(j) - height(j) // 32 * 16)
        return (0, cut) if way == PLUS else (cut, height(j) - cut)

    def index_of(way, k):
        return 10 if k == HALF_RING else way * 5 + k - 1

    def w_at(slot):
        return wts_all.at[pl.ds(0, no_block), pl.ds(pl.multiple_of(slot * 8, 8), 8), :]

    def gather_w(i, slot, to, src=None):
        return send(w_at(slot) if src is None else src, w_at(slot), gws.at[i], gwr.at[i], row=to)

    def gather_z(way, k, j):
        step = 1 if way == PLUS else -1
        slot = col_of(j, -step * (k - 1))
        src = feat if (j == 0 and k == 1) else feat_all.at[slot]
        dst = feat_all.at[slot]
        if k == HALF_RING or j != 0:
            part = pl.ds(*(share(way, j) if k == HALF_RING else (0, ringed)))
            src, dst = src.at[part], dst.at[part]
        return send(src, dst, gzs.at[way, k - 1, j], gzr.at[way, k - 1, j], col=col_of(0, step))

    enter(col_of, row_of)
    core_to, h_to = row_of(0, 0, 1), row_of(0, 1, 0)
    x_up, x_down = row_of(1, 0, 0), row_of(-1, 0, 0)

    zc = {}
    yc = {}
    for way in (PLUS, MINUS):
        zc[way, 1, 0] = gather_z(way, 1, 0)
    for j in (1, 3, 2):
        yc[j] = send(feat, feat_all.at[me_col], gys.at[j - 1], gyr.at[j - 1], col=col_of(4 - j, 0))
    w_up = gather_w(1, me_row, x_up, wts)
    w_down = gather_w(2, me_row, x_down, wts)
    cores = [gather_w(7, me_row, core_to, wts)]
    mine = pltpu.make_async_copy(wts, w_at(me_row), local_sem)
    mine.start()
    feat_all[me_col] = feat[...]
    wts_all[no_block] = jnp.zeros_like(wts_all[no_block])

    w_h = None
    wc = {}

    def w_stage_x():
        w_up.wait_recv()
        slot = row_of(-1, 0, 0)
        wc["first"] = gather_w(3, slot, x_up)
        cores.append(gather_w(8, slot, core_to))
        w_down.wait_recv()
        cores.append(gather_w(9, row_of(1, 0, 0), core_to))

    def w_stage_h():
        w_h.wait_recv()
        slot = row_of(0, 1, 0)
        wc["up"] = gather_w(4, slot, x_up)
        wc["down"] = gather_w(5, slot, x_down)
        cores.append(gather_w(10, slot, core_to))
        wc["first"].wait_recv()
        cores.append(gather_w(13, row_of(2, 0, 0), core_to))

    def w_stage_far():
        wc["down"].wait_recv()
        slot = row_of(1, 1, 0)
        wc["last"] = gather_w(6, slot, x_down)
        cores.append(gather_w(11, slot, core_to))
        wc["up"].wait_recv()
        cores.append(gather_w(12, row_of(-1, 1, 0), core_to))

    def w_stage_last():
        wc["last"].wait_recv()
        cores.append(gather_w(14, row_of(2, 1, 0), core_to))

    def find_blocks(b, carry):
        for f in range(columns):
            found = jnp.int32(no_block)
            for s in range(slots):
                found = jnp.where(rows[f, s] == b, jnp.int32(f * slots + s), found)
            places_of[b, f] = found
        return carry

    quarter = Y * Z // 4
    spread = []

    def spread_y(way, k):
        slot = col_of(0, -k if way == PLUS else k)
        part = feat_all.at[slot].at[pl.ds(ringed, SPREAD)]
        i = index_of(way, k)
        for d in (1, 3, 2):
            spread.append(
                send(part, part, gss.at[i, d - 1], gsr.at[i, d - 1], col=col_of(d, 0))
            )

    def pass_on(k, j):
        for way in (PLUS, MINUS):
            zc[way, k, j].wait_recv()
            if k < HALF_RING:
                zc[way, k + 1, j] = gather_z(way, k + 1, j)
            if j == 0 and (k < HALF_RING or way == MINUS):
                spread_y(way, k)

    def begin(j):
        yc[j].wait_recv()
        for way in (PLUS, MINUS):
            zc[way, 1, j] = gather_z(way, 1, j)

    pass_on(1, 0)
    begin(1)
    begin(3)
    pass_on(2, 0)
    begin(2)
    w_h = gather_w(0, me_row, h_to, wts)
    stages = {1: w_stage_x, 2: w_stage_h, 3: w_stage_far, 4: w_stage_last}
    for k in range(1, HALF_RING):
        if k + 2 <= HALF_RING:
            pass_on(k + 2, 0)
        for j in (1, 3, 2):
            pass_on(k, j)
        if k in stages:
            stages[k]()
            lax.fori_loop((k - 1) * quarter, k * quarter, find_blocks, 0)
    mine.wait()
    for copy in cores:
        copy.wait_recv()
    for j in range(1, Y):
        for way in (PLUS, MINUS):
            zc[way, HALF_RING, j].wait_recv()
    for copy in spread:
        copy.wait_recv()

    def pick(f):
        return jnp.concatenate([feat_all[rows[f, s]] for s in range(slots)], axis=0)

    c = math.sqrt(2.0 / math.pi)
    for f in range(columns):
        w = wts_all[f * slots : (f + 1) * slots].reshape(slots * 128, 128)
        v = lax.dot_general(w, pick(f), (((0,), (0,)), ((), ())), preferred_element_type=f32)
        sq = v * v
        t = jnp.tanh(c * (v + 0.044715 * (sq * v)))
        gate = 0.5 * (1.0 + t)
        here = pl.ds(f * 128, 128)
        hidden[here, :] = (v * gate).astype(bf16)
        slope = gate + 0.5 * v * (1.0 - t * t) * (c * (1.0 + (3 * 0.044715) * sq))
        grad[here, :] = (upper[here, :].astype(f32) * slope).astype(bf16)

    order = (2, 1, 3, 0)
    others = order[:-1]

    def terms(way, k, dz):
        left = []
        for j in order:
            b = col_of(j, dz)
            left.append(
                jnp.concatenate([wts_all[places_of[b, f]] for f in range(columns)], axis=1)
            )
        term[way, k % 2] = jnp.dot(jnp.concatenate(left, axis=0), grad[...], preferred_element_type=f32)

    def term_of(way, k, j, start=0, size=128):
        return term[way, k % 2, pl.ds(order.index(j) * 128 + start, size), :]

    def send_z(way, k, j):
        step = 1 if way == PLUS else -1
        part = pl.ds(*(share(way, j) if k == 0 else (0, height(j))))
        return send(
            zbuf_s.at[way, k, j, part], zbuf_r.at[way, k, j, part],
            zs.at[way, k, j], zr.at[way, k, j], col=col_of(0, step),
        )

    def send_x(i, to):
        return send(xbuf_s.at[i], xbuf_r.at[i], xs.at[i], xr.at[i], row=to)

    zc = {}
    sc = {}

    def send_spread(way, k):
        i = index_of(way, HALF_RING - k)
        for j in others:
            sbuf_s[i, j - 1] = term_of(way, k, j, ringed, SPREAD).astype(bf16)
            sc[i, j] = send(
                sbuf_s.at[i, j - 1], sbuf_r.at[i, j - 1],
                ss.at[i, j - 1], sr.at[i, j - 1], col=col_of(j, 0),
            )

    def own_term(way, k, start, size):
        value = term_of(way, k, 0, start, size)
        if start + size < whole:
            return [(start, size, value)]
        i = index_of(way, HALF_RING - k)
        for j in others:
            sc[i, j].wait_recv()
        last = value[ringed - start :]
        for j in others:
            last = last + sbuf_r[i, j - 1].astype(f32)
        return [(start, ringed - start, value[: ringed - start]), (ringed, SPREAD, last)]

    def put(way, k, j, source, start, size, arrived):
        pieces = (
            own_term(source, k, start, size)
            if j == 0
            else [(start, size, term_of(source, k, j, start, size))]
        )
        for at, n, value in pieces:
            if arrived:
                value = value + zbuf_r[way, k - 1, j, pl.ds(at, n), :].astype(f32)
            zbuf_s[way, k, j, pl.ds(at, n), :] = value.astype(bf16)

    def first_z(j):
        for way in (PLUS, MINUS):
            put(way, 0, j, PLUS, *share(way, j), False)
            zc[way, 0, j] = send_z(way, 0, j)

    terms(PLUS, 0, HALF_RING)
    for j in others:
        first_z(j)
    send_spread(PLUS, 0)

    for f in range(columns):
        wg = lax.dot_general(
            pick(f), grad[pl.ds(f * 128, 128), :], (((1,), (1,)), ((), ())),
            preferred_element_type=f32,
        )
        for s in range(slots):
            w_part[:, pl.ds((f * slots + s) * 8, 8), :] = wg[s * 128 : (s + 1) * 128].reshape(
                X * 4, 8, 128
            )

    dests = [(2, 0), (2, 1), (1, 0), (1, 1), (-1, 0), (-1, 1), (0, 1), (0, 0)]
    cc = []
    for i, (dx, dh) in enumerate(dests):
        cbuf_s[i] = w_part[row_of(dx, dh, 1)].astype(bf16)
        cc.append(send(cbuf_s.at[i], cbuf_r.at[i], cs.at[i], cr.at[i], row=core_to))

    def pair(i):
        dx, dh = dests[i]
        cc[i].wait_recv()
        return w_part[row_of(dx, dh, 0)] + cbuf_r[i].astype(f32)

    xc = {}

    def w_far():
        xbuf_s[0] = pair(0).astype(bf16)
        xc[0] = send_x(0, x_up)
        xbuf_s[1] = pair(1).astype(bf16)
        xc[1] = send_x(1, x_down)
        xbuf_s[2] = pair(3).astype(bf16)
        xc[2] = send_x(2, x_up)
        xbuf_s[3] = pair(4).astype(bf16)
        xc[3] = send_x(3, x_down)

    def w_near():
        xc[0].wait_recv()
        xbuf_s[4] = (pair(2) + xbuf_r[0].astype(f32)).astype(bf16)
        xc[4] = send_x(4, x_up)
        xc[1].wait_recv()
        xbuf_s[5] = (pair(5) + xbuf_r[1].astype(f32)).astype(bf16)
        xc[5] = send_x(5, x_down)
        own[...] = pair(7)

    def w_across():
        xc[2].wait_recv()
        xc[5].wait_recv()
        total = pair(6) + xbuf_r[2].astype(f32) + xbuf_r[5].astype(f32)
        xbuf_s[6] = total.astype(bf16)
        xc[6] = send_x(6, h_to)

    def w_end():
        xc[3].wait_recv()
        xc[4].wait_recv()
        xc[6].wait_recv()
        total = own[...] + xbuf_r[3].astype(f32) + xbuf_r[4].astype(f32) + xbuf_r[6].astype(f32)
        w_out[...] = total * scale

    def add_z(k, j):
        for way in (PLUS, MINUS):
            zc[way, k - 1, j].wait_recv()
            if k > 1:
                put(way, k, j, way, 0, height(j), True)
            elif way == PLUS:
                put(way, k, j, way, *share(PLUS, j), True)
                put(way, k, j, way, *share(MINUS, j), False)
            else:
                put(way, k, j, way, *share(PLUS, j), False)
                put(way, k, j, way, *share(MINUS, j), True)
            zc[way, k, j] = send_z(way, k, j)

    stages = {1: w_far, 2: w_near, 3: w_across, 4: w_end}
    for k in range(1, HALF_RING):
        terms(PLUS, k, HALF_RING - k)
        terms(MINUS, k, k - HALF_RING)
        send_spread(PLUS, k)
        send_spread(MINUS, k)
        for j in others:
            add_z(k, j)
        if k == 1:
            first_z(0)
        else:
            add_z(k - 1, 0)
        if k in stages:
            stages[k]()
    last = HALF_RING - 1
    terms(PLUS, last + 1, 0)
    add_z(last, 0)

    def total_z(j):
        for way in (PLUS, MINUS):
            zc[way, last, j].wait_recv()
        return (
            term_of(PLUS, last + 1, j, 0, height(j))
            + zbuf_r[PLUS, last, j, pl.ds(0, height(j)), :].astype(f32)
            + zbuf_r[MINUS, last, j, pl.ds(0, height(j)), :].astype(f32)
        )

    yc = []
    for j in (2, 1, 3):
        ybuf_s[j - 1, pl.ds(0, ringed), :] = total_z(j).astype(bf16)
        ybuf_s[j - 1, pl.ds(ringed, SPREAD), :] = term_of(
            PLUS, last + 1, j, ringed, SPREAD
        ).astype(bf16)
        yc.append(
            send(ybuf_s.at[j - 1], ybuf_r.at[j - 1], ys.at[j - 1], yr.at[j - 1], col=col_of(j, 0))
        )
    total = total_z(0)
    for copy in yc:
        copy.wait_recv()
    for j in range(Y - 1):
        total = total + ybuf_r[j].astype(f32)
    in_out[...] = total.astype(bf16)
    for copy in started:
        copy.wait_send()


def step(rows, features, weights, upper, scale):
    dma = pltpu.SemaphoreType.DMA
    bf16, f32 = jnp.bfloat16, jnp.float32
    block = features.shape
    pieces, side, n = weights.shape
    columns = rows.shape[0]
    piece = (pieces * side, n)
    ring = (2, HALF_RING, Y)
    spread = (Z - 1, Y - 1, SPREAD, block[1])
    vmem = pl.BlockSpec(memory_space=VMEM)
    return pl.pallas_call(
        functools.partial(step_kernel, scale),
        out_shape=(
            jax.ShapeDtypeStruct(upper.shape, bf16),
            jax.ShapeDtypeStruct(block, bf16),
            jax.ShapeDtypeStruct(piece, f32),
        ),
        in_specs=[pl.BlockSpec(memory_space=pltpu.SMEM), vmem, vmem, vmem],
        out_specs=(vmem,) * 3,
        scratch_shapes=[
            VMEM((Y * Z,) + block, bf16),
            VMEM((pieces + 1, X * 4 * side, n), bf16),
            pltpu.SMEM((Y * Z, columns), jnp.int32),
            VMEM(upper.shape, bf16),
            VMEM((2, 2, Y * block[0], block[1]), f32),
            VMEM((X * 4,) + piece, f32),
            VMEM(ring + block, bf16), VMEM(ring + block, bf16),
            VMEM((Y - 1,) + block, bf16), VMEM((Y - 1,) + block, bf16),
            VMEM((8,) + piece, bf16), VMEM((8,) + piece, bf16),
            VMEM(piece, f32),
            VMEM((7,) + piece, bf16), VMEM((7,) + piece, bf16),
            VMEM(spread, bf16), VMEM(spread, bf16),
            dma((Y - 1,)), dma((Y - 1,)),
            dma(ring), dma(ring),
            dma((15,)), dma((15,)),
            dma(spread[:2]), dma(spread[:2]),
            dma,
            dma(ring), dma(ring),
            dma((Y - 1,)), dma((Y - 1,)),
            dma((8,)), dma((8,)),
            dma((7,)), dma((7,)),
            dma(spread[:2]), dma(spread[:2]),
        ],
        compiler_params=pltpu.CompilerParams(collective_id=1, has_side_effects=True),
        name="layer_and_gradients",
    )(rows, features, weights, upper)


def finish_kernel(hidden, in_grad, w_grad, hidden_out, in_out, w_out):
    hidden_out[...] = hidden[...]
    in_out[...] = in_grad[...]
    w_out[...] = w_grad[...]


def finish(*arrays):
    return pl.pallas_call(
        finish_kernel,
        out_shape=tuple(jax.ShapeDtypeStruct(a.shape, a.dtype) for a in arrays),
        in_specs=[pl.BlockSpec(memory_space=VMEM)] * 3,
        out_specs=(pl.BlockSpec(memory_space=VMEM),) * 3,
        name="outputs",
    )(*arrays)


def local(features, weight_blocks, block_rows, upstream):
    grad_scale = float(features.shape[1] * lax.axis_size("row")) ** (-0.5)
    weights = weight_blocks.reshape((-1,) + weight_blocks.shape[2:])
    hidden, input_grad, w_grad = finish(
        *step(block_rows, features, weights, upstream, grad_scale)
    )
    return (hidden, input_grad, w_grad.reshape(weight_blocks.shape))


def solution(mesh):
    return jax.shard_map(
        local,
        mesh=mesh,
        in_specs=(P("col", "row"), P("col", None, "row", None), P("col", None), P("col", "row")),
        out_specs=(P("col", "row"), P("col", "row"), P("col", None, "row", None)),
        check_vma=False,
    )
```

```python
import functools
import math

import jax
import jax.numpy as jnp
from jax import lax
from jax.experimental import pallas as pl
from jax.experimental.pallas import tpu as pltpu
from jax.sharding import PartitionSpec as P

Y, Z = 4, 12
X = 4
HALF_RING = Z // 2
PLUS, MINUS = 0, 1
SPREAD = 32
VMEM = pltpu.VMEM


def places():
    col = lax.axis_index("col")
    row = lax.axis_index("row")
    y, z = col // Z, col % Z
    x, h, core = row // 4, (row // 2) % 2, row % 2

    def col_of(dy, dz):
        return ((y + dy + Y) % Y) * Z + (z + dz + Z) % Z

    def row_of(dx, dh, dc):
        return (((x + dx + X) % X) * 2 + (h + dh) % 2) * 2 + (core + dc) % 2

    return col_of, row_of


def enter(col_of, row_of):
    barrier = pltpu.get_barrier_semaphore()
    cols = [col_of(1, 0), col_of(2, 0), col_of(3, 0), col_of(0, 1), col_of(0, -1)]
    rows = [row_of(0, 0, 1), row_of(0, 1, 0), row_of(1, 0, 0), row_of(-1, 0, 0)]
    for c in cols:
        pl.semaphore_signal(barrier, inc=1, device_id={"col": c})
    for r in rows:
        pl.semaphore_signal(barrier, inc=1, device_id={"row": r})
    pl.semaphore_wait(barrier, len(cols) + len(rows))


def step_kernel(
    scale, rows, feat, wts, upper, hidden, in_out, w_out,
    feat_all, wts_all, places_of, grad, term, w_part,
    zbuf_s, zbuf_r, ybuf_s, ybuf_r, cbuf_s, cbuf_r, own, xbuf_s, xbuf_r,
    sbuf_s, sbuf_r,
    gys, gyr, gzs, gzr, gws, gwr, gss, gsr, local_sem,
    zs, zr, ys, yr, cs, cr, xs, xr, ss, sr,
):
    col_of, row_of = places()
    me_col, me_row = col_of(0, 0), row_of(0, 0, 0)
    whole = feat.shape[0]
    ringed = whole - SPREAD
    f32, bf16 = jnp.float32, jnp.bfloat16
    columns, slots = rows.shape
    no_block = columns * slots
    started = []

    def send(src, dst, send_sem, recv_sem, **to):
        copy = pltpu.make_async_remote_copy(
            src_ref=src, dst_ref=dst, send_sem=send_sem, recv_sem=recv_sem, device_id=to
        )
        copy.start()
        started.append(copy)
        return copy

    def height(j):
        return whole if j == 0 else ringed

    def share(way, j):
        cut = min(whole // 2, height(j) - height(j) // 32 * 16)
        return (0, cut) if way == PLUS else (cut, height(j) - cut)

    def index_of(way, k):
        return 10 if k == HALF_RING else way * 5 + k - 1

    def w_at(slot):
        return wts_all.at[pl.ds(0, no_block), pl.ds(pl.multiple_of(slot * 8, 8), 8), :]

    def gather_w(i, slot, to, src=None):
        return send(w_at(slot) if src is None else src, w_at(slot), gws.at[i], gwr.at[i], row=to)

    def gather_z(way, k, j):
        step = 1 if way == PLUS else -1
        slot = col_of(j, -step * (k - 1))
        src = feat if (j == 0 and k == 1) else feat_all.at[slot]
        dst = feat_all.at[slot]
        if k == HALF_RING or j != 0:
            part = pl.ds(*(share(way, j) if k == HALF_RING else (0, ringed)))
            src, dst = src.at[part], dst.at[part]
        return send(src, dst, gzs.at[way, k - 1, j], gzr.at[way, k - 1, j], col=col_of(0, step))

    enter(col_of, row_of)
    core_to, h_to = row_of(0, 0, 1), row_of(0, 1, 0)
    x_up, x_down = row_of(1, 0, 0), row_of(-1, 0, 0)

    zc = {}
    yc = {}
    for way in (PLUS, MINUS):
        zc[way, 1, 0] = gather_z(way, 1, 0)
    for j in (1, 3, 2):
        yc[j] = send(feat, feat_all.at[me_col], gys.at[j - 1], gyr.at[j - 1], col=col_of(4 - j, 0))
    w_up = gather_w(1, me_row, x_up, wts)
    w_down = gather_w(2, me_row, x_down, wts)
    cores = [gather_w(7, me_row, core_to, wts)]
    mine = pltpu.make_async_copy(wts, w_at(me_row), local_sem)
    mine.start()
    feat_all[me_col] = feat[...]
    wts_all[no_block] = jnp.zeros_like(wts_all[no_block])

    w_h = None
    wc = {}

    def w_stage_x():
        w_up.wait_recv()
        slot = row_of(-1, 0, 0)
        wc["first"] = gather_w(3, slot, x_up)
        cores.append(gather_w(8, slot, core_to))
        w_down.wait_recv()
        cores.append(gather_w(9, row_of(1, 0, 0), core_to))

    def w_stage_h():
        w_h.wait_recv()
        slot = row_of(0, 1, 0)
        wc["up"] = gather_w(4, slot, x_up)
        wc["down"] = gather_w(5, slot, x_down)
        cores.append(gather_w(10, slot, core_to))
        wc["first"].wait_recv()
        cores.append(gather_w(13, row_of(2, 0, 0), core_to))

    def w_stage_far():
        wc["down"].wait_recv()
        slot = row_of(1, 1, 0)
        wc["last"] = gather_w(6, slot, x_down)
        cores.append(gather_w(11, slot, core_to))
        wc["up"].wait_recv()
        cores.append(gather_w(12, row_of(-1, 1, 0), core_to))

    def w_stage_last():
        wc["last"].wait_recv()
        cores.append(gather_w(14, row_of(2, 1, 0), core_to))

    def find_blocks(b, carry):
        for f in range(columns):
            found = jnp.int32(no_block)
            for s in range(slots):
                found = jnp.where(rows[f, s] == b, jnp.int32(f * slots + s), found)
            places_of[b, f] = found
        return carry

    quarter = Y * Z // 4
    spread = []

    def spread_y(way, k):
        slot = col_of(0, -k if way == PLUS else k)
        part = feat_all.at[slot].at[pl.ds(ringed, SPREAD)]
        i = index_of(way, k)
        for d in (1, 3, 2):
            spread.append(
                send(part, part, gss.at[i, d - 1], gsr.at[i, d - 1], col=col_of(d, 0))
            )

    def pass_on(k, j):
        for way in (PLUS, MINUS):
            zc[way, k, j].wait_recv()
            if k < HALF_RING:
                zc[way, k + 1, j] = gather_z(way, k + 1, j)
        if j == 0 and k > 2:
            spread_both(k)

    def spread_both(k):
        for way in (PLUS, MINUS) if k < HALF_RING else (MINUS,):
            spread_y(way, k)

    def begin(j):
        yc[j].wait_recv()
        for way in (PLUS, MINUS):
            zc[way, 1, j] = gather_z(way, 1, j)

    pass_on(1, 0)
    begin(1)
    begin(3)
    pass_on(2, 0)
    begin(2)
    spread_both(1)
    spread_both(2)
    w_h = gather_w(0, me_row, h_to, wts)
    stages = {1: w_stage_x, 2: w_stage_h, 3: w_stage_far, 4: w_stage_last}
    for k in range(1, HALF_RING):
        if k + 2 <= HALF_RING:
            pass_on(k + 2, 0)
        for j in (1, 3, 2):
            pass_on(k, j)
        if k in stages:
            stages[k]()
            lax.fori_loop((k - 1) * quarter, k * quarter, find_blocks, 0)
    mine.wait()
    for copy in cores:
        copy.wait_recv()
    for j in range(1, Y):
        for way in (PLUS, MINUS):
            zc[way, HALF_RING, j].wait_recv()
    for copy in spread:
        copy.wait_recv()

    def pick(f):
        return jnp.concatenate([feat_all[rows[f, s]] for s in range(slots)], axis=0)

    c = math.sqrt(2.0 / math.pi)
    for f in range(columns):
        w = wts_all[f * slots : (f + 1) * slots].reshape(slots * 128, 128)
        v = lax.dot_general(w, pick(f), (((0,), (0,)), ((), ())), preferred_element_type=f32)
        sq = v * v
        t = jnp.tanh(c * (v + 0.044715 * (sq * v)))
        gate = 0.5 * (1.0 + t)
        here = pl.ds(f * 128, 128)
        hidden[here, :] = (v * gate).astype(bf16)
        slope = gate + 0.5 * v * (1.0 - t * t) * (c * (1.0 + (3 * 0.044715) * sq))
        grad[here, :] = (upper[here, :].astype(f32) * slope).astype(bf16)

    order = (2, 1, 3, 0)
    others = order[:-1]

    def terms(way, k, dz):
        left = []
        for j in order:
            b = col_of(j, dz)
            left.append(
                jnp.concatenate([wts_all[places_of[b, f]] for f in range(columns)], axis=1)
            )
        term[way, k % 2] = jnp.dot(jnp.concatenate(left, axis=0), grad[...], preferred_element_type=f32)

    def term_of(way, k, j, start=0, size=128):
        return term[way, k % 2, pl.ds(order.index(j) * 128 + start, size), :]

    def send_z(way, k, j):
        step = 1 if way == PLUS else -1
        part = pl.ds(*(share(way, j) if k == 0 else (0, height(j))))
        return send(
            zbuf_s.at[way, k, j, part], zbuf_r.at[way, k, j, part],
            zs.at[way, k, j], zr.at[way, k, j], col=col_of(0, step),
        )

    def send_x(i, to):
        return send(xbuf_s.at[i], xbuf_r.at[i], xs.at[i], xr.at[i], row=to)

    zc = {}
    sc = {}

    def send_spread(way, k):
        i = index_of(way, HALF_RING - k)
        for j in others:
            sbuf_s[i, j - 1] = term_of(way, k, j, ringed, SPREAD).astype(bf16)
            sc[i, j] = send(
                sbuf_s.at[i, j - 1], sbuf_r.at[i, j - 1],
                ss.at[i, j - 1], sr.at[i, j - 1], col=col_of(j, 0),
            )

    def own_term(way, k, start, size):
        value = term_of(way, k, 0, start, size)
        if start + size < whole:
            return [(start, size, value)]
        i = index_of(way, HALF_RING - k)
        for j in others:
            sc[i, j].wait_recv()
        last = value[ringed - start :]
        for j in others:
            last = last + sbuf_r[i, j - 1].astype(f32)
        return [(start, ringed - start, value[: ringed - start]), (ringed, SPREAD, last)]

    def put(way, k, j, source, start, size, arrived):
        pieces = (
            own_term(source, k, start, size)
            if j == 0
            else [(start, size, term_of(source, k, j, start, size))]
        )
        for at, n, value in pieces:
            if arrived:
                value = value + zbuf_r[way, k - 1, j, pl.ds(at, n), :].astype(f32)
            zbuf_s[way, k, j, pl.ds(at, n), :] = value.astype(bf16)

    def first_z(j):
        for way in (PLUS, MINUS):
            put(way, 0, j, PLUS, *share(way, j), False)
            zc[way, 0, j] = send_z(way, 0, j)

    terms(PLUS, 0, HALF_RING)
    for j in others:
        first_z(j)
    send_spread(PLUS, 0)

    for f in range(columns):
        wg = lax.dot_general(
            pick(f), grad[pl.ds(f * 128, 128), :], (((1,), (1,)), ((), ())),
            preferred_element_type=f32,
        )
        for s in range(slots):
            w_part[:, pl.ds((f * slots + s) * 8, 8), :] = wg[s * 128 : (s + 1) * 128].reshape(
                X * 4, 8, 128
            )

    dests = [(2, 0), (2, 1), (1, 0), (1, 1), (-1, 0), (-1, 1), (0, 1), (0, 0)]
    cc = []
    for i, (dx, dh) in enumerate(dests):
        cbuf_s[i] = w_part[row_of(dx, dh, 1)].astype(bf16)
        cc.append(send(cbuf_s.at[i], cbuf_r.at[i], cs.at[i], cr.at[i], row=core_to))

    def pair(i):
        dx, dh = dests[i]
        cc[i].wait_recv()
        return w_part[row_of(dx, dh, 0)] + cbuf_r[i].astype(f32)

    xc = {}

    def w_far():
        xbuf_s[0] = pair(0).astype(bf16)
        xc[0] = send_x(0, x_up)
        xbuf_s[1] = pair(1).astype(bf16)
        xc[1] = send_x(1, x_down)
        xbuf_s[2] = pair(3).astype(bf16)
        xc[2] = send_x(2, x_up)
        xbuf_s[3] = pair(4).astype(bf16)
        xc[3] = send_x(3, x_down)

    def w_near():
        xc[0].wait_recv()
        xbuf_s[4] = (pair(2) + xbuf_r[0].astype(f32)).astype(bf16)
        xc[4] = send_x(4, x_up)
        xc[1].wait_recv()
        xbuf_s[5] = (pair(5) + xbuf_r[1].astype(f32)).astype(bf16)
        xc[5] = send_x(5, x_down)
        own[...] = pair(7)

    def w_across():
        xc[2].wait_recv()
        xc[5].wait_recv()
        total = pair(6) + xbuf_r[2].astype(f32) + xbuf_r[5].astype(f32)
        xbuf_s[6] = total.astype(bf16)
        xc[6] = send_x(6, h_to)

    def w_end():
        xc[3].wait_recv()
        xc[4].wait_recv()
        xc[6].wait_recv()
        total = own[...] + xbuf_r[3].astype(f32) + xbuf_r[4].astype(f32) + xbuf_r[6].astype(f32)
        w_out[...] = total * scale

    def add_z(k, j):
        for way in (PLUS, MINUS):
            zc[way, k - 1, j].wait_recv()
            if k > 1:
                put(way, k, j, way, 0, height(j), True)
            elif way == PLUS:
                put(way, k, j, way, *share(PLUS, j), True)
                put(way, k, j, way, *share(MINUS, j), False)
            else:
                put(way, k, j, way, *share(PLUS, j), False)
                put(way, k, j, way, *share(MINUS, j), True)
            zc[way, k, j] = send_z(way, k, j)

    stages = {1: w_far, 2: w_near, 3: w_across, 4: w_end}
    for k in range(1, HALF_RING):
        terms(PLUS, k, HALF_RING - k)
        terms(MINUS, k, k - HALF_RING)
        send_spread(PLUS, k)
        send_spread(MINUS, k)
        for j in others:
            add_z(k, j)
        if k == 1:
            first_z(0)
        else:
            add_z(k - 1, 0)
        if k in stages:
            stages[k]()
    last = HALF_RING - 1
    terms(PLUS, last + 1, 0)
    add_z(last, 0)

    def total_z(j):
        for way in (PLUS, MINUS):
            zc[way, last, j].wait_recv()
        return (
            term_of(PLUS, last + 1, j, 0, height(j))
            + zbuf_r[PLUS, last, j, pl.ds(0, height(j)), :].astype(f32)
            + zbuf_r[MINUS, last, j, pl.ds(0, height(j)), :].astype(f32)
        )

    yc = []
    for j in (2, 1, 3):
        ybuf_s[j - 1, pl.ds(0, ringed), :] = total_z(j).astype(bf16)
        ybuf_s[j - 1, pl.ds(ringed, SPREAD), :] = term_of(
            PLUS, last + 1, j, ringed, SPREAD
        ).astype(bf16)
        yc.append(
            send(ybuf_s.at[j - 1], ybuf_r.at[j - 1], ys.at[j - 1], yr.at[j - 1], col=col_of(j, 0))
        )
    total = total_z(0)
    for copy in yc:
        copy.wait_recv()
    for j in range(Y - 1):
        total = total + ybuf_r[j].astype(f32)
    in_out[...] = total.astype(bf16)
    for copy in started:
        copy.wait_send()


def step(rows, features, weights, upper, scale):
    dma = pltpu.SemaphoreType.DMA
    bf16, f32 = jnp.bfloat16, jnp.float32
    block = features.shape
    pieces, side, n = weights.shape
    columns = rows.shape[0]
    piece = (pieces * side, n)
    ring = (2, HALF_RING, Y)
    spread = (Z - 1, Y - 1, SPREAD, block[1])
    vmem = pl.BlockSpec(memory_space=VMEM)
    return pl.pallas_call(
        functools.partial(step_kernel, scale),
        out_shape=(
            jax.ShapeDtypeStruct(upper.shape, bf16),
            jax.ShapeDtypeStruct(block, bf16),
            jax.ShapeDtypeStruct(piece, f32),
        ),
        in_specs=[pl.BlockSpec(memory_space=pltpu.SMEM), vmem, vmem, vmem],
        out_specs=(vmem,) * 3,
        scratch_shapes=[
            VMEM((Y * Z,) + block, bf16),
            VMEM((pieces + 1, X * 4 * side, n), bf16),
            pltpu.SMEM((Y * Z, columns), jnp.int32),
            VMEM(upper.shape, bf16),
            VMEM((2, 2, Y * block[0], block[1]), f32),
            VMEM((X * 4,) + piece, f32),
            VMEM(ring + block, bf16), VMEM(ring + block, bf16),
            VMEM((Y - 1,) + block, bf16), VMEM((Y - 1,) + block, bf16),
            VMEM((8,) + piece, bf16), VMEM((8,) + piece, bf16),
            VMEM(piece, f32),
            VMEM((7,) + piece, bf16), VMEM((7,) + piece, bf16),
            VMEM(spread, bf16), VMEM(spread, bf16),
            dma((Y - 1,)), dma((Y - 1,)),
            dma(ring), dma(ring),
            dma((15,)), dma((15,)),
            dma(spread[:2]), dma(spread[:2]),
            dma,
            dma(ring), dma(ring),
            dma((Y - 1,)), dma((Y - 1,)),
            dma((8,)), dma((8,)),
            dma((7,)), dma((7,)),
            dma(spread[:2]), dma(spread[:2]),
        ],
        compiler_params=pltpu.CompilerParams(collective_id=1, has_side_effects=True),
        name="layer_and_gradients",
    )(rows, features, weights, upper)


def finish_kernel(hidden, in_grad, w_grad, hidden_out, in_out, w_out):
    hidden_out[...] = hidden[...]
    in_out[...] = in_grad[...]
    w_out[...] = w_grad[...]


def finish(*arrays):
    return pl.pallas_call(
        finish_kernel,
        out_shape=tuple(jax.ShapeDtypeStruct(a.shape, a.dtype) for a in arrays),
        in_specs=[pl.BlockSpec(memory_space=VMEM)] * 3,
        out_specs=(pl.BlockSpec(memory_space=VMEM),) * 3,
        name="outputs",
    )(*arrays)


def local(features, weight_blocks, block_rows, upstream):
    grad_scale = float(features.shape[1] * lax.axis_size("row")) ** (-0.5)
    weights = weight_blocks.reshape((-1,) + weight_blocks.shape[2:])
    hidden, input_grad, w_grad = finish(
        *step(block_rows, features, weights, upstream, grad_scale)
    )
    return (hidden, input_grad, w_grad.reshape(weight_blocks.shape))


def solution(mesh):
    return jax.shard_map(
        local,
        mesh=mesh,
        in_specs=(P("col", "row"), P("col", None, "row", None), P("col", None), P("col", "row")),
        out_specs=(P("col", "row"), P("col", "row"), P("col", None, "row", None)),
        check_vma=False,
    )
```
